512 devices in a mesh: group: 64 (over x_lo, z, core), shard: 8 (over y, x_hi).
Axes of the slice: x: 4 (x_hi: 2, x_lo: 2; x = x_hi * 2 + x_lo), y: 4, z: 16, core: 2. Of those that a mesh axis runs over, the one named last changes fastest.
Arguments:
- prompts: bfloat16 [512, 128, 1280], P(('group', 'shard')), may hold values from -6 to 6
- lengths: int32 [512], P(('group', 'shard')), may hold values from 32 to 128
- qkv_master: float32 [1280, 1920], P('group', 'shard')
- out_master: float32 [1280, 1280], P('group', 'shard'), may hold values from -0.15625 to 0.15625
- gate_up_master: float32 [1280, 2, 3584], P('group', None, 'shard'), may hold values from -0.15625 to 0.15625
- down_weight: bfloat16 [3584, 1280], P('shard'), may hold values from -0.09375 to 0.09375
- attn_gain: float32 [1280], replicated, may hold values from 0.25 to 1.75
- mlp_gain: float32 [1280], replicated, may hold values from 0.25 to 1.75
Outputs:
- hidden: bfloat16 [512, 128, 1280], P(('group', 'shard'))
- cache: bfloat16 [512, 128, 640], P(('group', 'shard'))
The draws below stay inside these ranges and needn't reach their ends.
Inputs may be any that keep to these rules, and one draw needn't show every extreme that they name: `lengths`: live tokens of each prompt; positions from the length on are padding.
All inputs are finite; a program needn't handle non-finite values.
Results may differ from the reference program's by a relative error of at most 0.013.
The reference program's roundings to bfloat16 on the way count: a program that leaves them out, or rounds other values in their place, can miss the bound.
Values may be sent and summed in bfloat16 or wider, within the bound.
No kernel may reach another device: no remote copies, remote signals or barrier semaphores. Data moves between devices by JAX's collectives and lax.ppermute only.
A program may use at most 64 MiB of HBM per device.

```python
import jax
import jax.numpy as jnp
from jax import lax

D = 1280
QUERY_HEADS = 20
KEY_VALUE_HEADS = 5
HEAD_SIZE = 64
FF = 3584
LMAX = 128
QKVW = 1920
REQS = 512
N_SHARD = 8


def draw_qkv_master(key, part):
    base = jax.random.normal(jax.random.fold_in(key, 11), (D, QKVW), jnp.float32) * D ** (-0.5)
    return base


def set_ends(values, rng, least, high):
    spot = [jax.random.randint(jax.random.fold_in(rng, axis), (), 0, length) for axis, length in enumerate(values.shape)]
    main_axis = values.shape.index(max(values.shape))
    beside = spot[:main_axis] + [(spot[main_axis] + 1) % values.shape[main_axis]] + spot[main_axis + 1:]
    return values.at[tuple(spot)].set(least).at[tuple(beside)].set(high)


def steps_of(stream_key, extent, pieces, low, high):
    factor_of = 1.0
    for axis_at, blocks in pieces:
        draws = jax.random.uniform(jax.random.fold_in(jax.random.fold_in(stream_key, 6), axis_at), (blocks,), jnp.float32, low / len(pieces), high / len(pieces))
        factor_of = factor_of * jnp.repeat(jnp.exp(draws), extent[axis_at] // blocks).reshape((-1,) + (1,) * (len(extent) - 1 - axis_at))
    return factor_of


def scatter_about(stream_key, shape, spread, limit, cuts=(), held_as=jnp.bfloat16):
    drawn = spread * jax.random.normal(stream_key, shape, jnp.float32)
    if cuts:
        drawn = drawn * steps_of(stream_key, shape, cuts, -0.22, 0.18)
    return jnp.clip(drawn, -limit, limit).astype(held_as)


def setup_inputs(seed: int = 0) -> dict:
    seeds = jax.random.split(jax.random.key(seed), 9)
    return {
        "prompts": scatter_about(seeds[0], (REQS, LMAX, D), 1.0, 6.0, ((0, 512),)),
        "lengths": set_ends(jax.random.randint(seeds[1], (REQS,), LMAX // 4, LMAX + 1), jax.random.fold_in(seeds[1], 1), LMAX // 4, LMAX).astype(jnp.int32),
        "qkv_master": draw_qkv_master(jax.random.fold_in(seeds[8], 71), 0),
        "out_master": scatter_about(seeds[3], (QUERY_HEADS * HEAD_SIZE, D), (QUERY_HEADS * HEAD_SIZE) ** -0.5, 0.15625, ((0, 64), (1, 8)), jnp.float32),
        "gate_up_master": scatter_about(seeds[4], (D, 2, FF), D ** -0.5, 0.15625, ((0, 64), (2, 8)), jnp.float32),
        "down_weight": scatter_about(seeds[5], (FF, D), FF ** -0.5, 0.09375, ((0, 8),)),
        "attn_gain": jnp.clip(1.0 + 0.15 * jax.random.normal(seeds[6], (D,), jnp.float32), 0.25, 1.75),
        "mlp_gain": jnp.clip(1.0 + 0.15 * jax.random.normal(seeds[7], (D,), jnp.float32), 0.25, 1.75),
    }


def norm_rows(stream, scale_gain):
    return stream * lax.rsqrt(lax.optimization_barrier(jnp.mean(stream * stream, axis=-1, keepdims=True)) + 1e-05) * scale_gain

def rotary(heads, positions):
    half_dim = heads.shape[-1] // 2
    frequency = 10000.0 ** (-(jnp.arange(half_dim).astype(heads.dtype) * 2.0 / heads.shape[-1]))
    angles = positions[:, None] * frequency[None, :]
    cosine = jnp.cos(angles)[:, None, :]
    sine_part = jnp.sin(angles)[:, None, :]
    first_half = heads[..., :half_dim]
    second_half = heads[..., half_dim:]
    return jnp.concatenate([first_half * cosine - second_half * sine_part, second_half * cosine + first_half * sine_part], axis=-1)

def attention(query_key_value, length):
    token_rows = query_key_value.shape[0]
    query = query_key_value[:, :QUERY_HEADS * HEAD_SIZE].astype(jnp.float32).reshape(token_rows, QUERY_HEADS, HEAD_SIZE)
    key_rows = query_key_value[:, QUERY_HEADS * HEAD_SIZE:(QUERY_HEADS + KEY_VALUE_HEADS) * HEAD_SIZE].astype(jnp.float32).reshape(token_rows, KEY_VALUE_HEADS, HEAD_SIZE)
    value_rows = query_key_value[:, (QUERY_HEADS + KEY_VALUE_HEADS) * HEAD_SIZE:].reshape(token_rows, KEY_VALUE_HEADS, HEAD_SIZE)
    positions = jnp.arange(token_rows).astype(jnp.float32)
    rotated_query = rotary(query, positions).astype(jnp.bfloat16)
    rotated_keys = rotary(key_rows, positions).astype(jnp.bfloat16)
    grouped_queries = rotated_query.reshape(token_rows, KEY_VALUE_HEADS, QUERY_HEADS // KEY_VALUE_HEADS, HEAD_SIZE)
    scores = jnp.einsum('qkgd,skd->kgqs', grouped_queries.astype(jnp.float32), rotated_keys.astype(jnp.float32)) * HEAD_SIZE ** (-0.5)
    indices = jnp.arange(token_rows).astype(jnp.int32)
    allowed = (indices[None, :] <= indices[:, None]) & (indices[None, :] < length)
    scores = jnp.where(allowed, scores, -1e+30)
    largest = lax.optimization_barrier(jnp.max(scores, axis=-1, keepdims=True))
    weights = jnp.exp(scores - largest)
    probability = (weights / lax.optimization_barrier(jnp.sum(weights, axis=-1, keepdims=True))).astype(jnp.bfloat16)
    attended = jnp.einsum('kgqs,skd->qkgd', probability.astype(jnp.float32), value_rows.astype(jnp.float32))
    return (attended.reshape(token_rows, QUERY_HEADS * HEAD_SIZE).astype(jnp.bfloat16), rotated_keys, value_rows)

def reference(prompts, lengths, qkv_master, out_master, gate_up_master, down_weight, attn_gain, mlp_gain):
    w_qkv = qkv_master.astype(jnp.bfloat16)
    w_out = out_master.astype(jnp.bfloat16)
    w_gate_up = gate_up_master.astype(jnp.bfloat16).reshape(D, 2 * FF)
    down_blocks = down_weight.reshape(N_SHARD, FF // N_SHARD, D).astype(jnp.float32)

    def one_request(item):
        tokens, length = item
        stream = tokens.astype(jnp.float32)
        token_rows = stream.shape[0]
        normed_in = norm_rows(stream, attn_gain).astype(jnp.bfloat16)
        query_key_value = jnp.dot(normed_in, w_qkv, preferred_element_type=jnp.float32).astype(jnp.bfloat16)
        attended, rotated_keys, value_rows = attention(query_key_value, length)
        middle = stream + jnp.dot(attended, w_out, preferred_element_type=jnp.float32)
        normed_mid = norm_rows(middle, mlp_gain).astype(jnp.bfloat16)
        gate_up = jnp.dot(normed_mid, w_gate_up, preferred_element_type=jnp.float32).reshape(token_rows, 2, FF)
        hidden_units = (jax.nn.silu(gate_up[:, 0]) * gate_up[:, 1]).astype(jnp.bfloat16)
        partial_sums = jnp.einsum('tnf,nfd->tnd', hidden_units.reshape(token_rows, N_SHARD, FF // N_SHARD).astype(jnp.float32), down_blocks).astype(jnp.bfloat16)
        partial_sums = lax.optimization_barrier(partial_sums)
        feed_out = lax.optimization_barrier(jnp.sum(partial_sums.astype(jnp.float32), axis=1))
        live_rows = (jnp.arange(token_rows).astype(jnp.int32) < length).astype(jnp.float32)[:, None]
        hidden = (live_rows * (middle + feed_out)).astype(jnp.bfloat16)
        joined_heads = jnp.concatenate([rotated_keys.reshape(token_rows, KEY_VALUE_HEADS * HEAD_SIZE).astype(jnp.float32), value_rows.reshape(token_rows, KEY_VALUE_HEADS * HEAD_SIZE).astype(jnp.float32)], axis=-1)
        cache = (live_rows * joined_heads).astype(jnp.bfloat16)
        return (hidden, cache)
    hidden, cache = lax.map(one_request, (prompts, lengths))
    return (hidden, cache)
```

```python
import jax
import jax.numpy as jnp
import numpy as np
from jax import lax
from jax.experimental import pallas as pl
from jax.experimental.pallas import tpu as pltpu
from jax.sharding import Mesh, PartitionSpec as P

QUERY_HEADS = 20
KEY_VALUE_HEADS = 5
HEAD_SIZE = 64
D = 1280
LMAX = 128
QW = 120
OW = 80
KHALF = 640
UNITS = 448
F32 = jnp.float32
BF16 = jnp.bfloat16

AXES = ("x_lo", "z", "core", "y", "x_hi")
SIZES = (2, 16, 2, 4, 2)


def tables():
    half_dim = HEAD_SIZE // 2
    frequency = np.float32(10000.0) ** (
        -(np.arange(half_dim).astype(np.float32) * np.float32(2.0) / np.float32(HEAD_SIZE))
    )
    angles = frequency.astype(np.float32)[:, None] * np.arange(LMAX).astype(np.float32)[None, :]
    return np.cos(angles).astype(np.float32), np.sin(angles).astype(np.float32)


def dot_nt(left, right):
    return lax.dot_general(left, right, (((1,), (1,)), ((), ())), preferred_element_type=F32)


def dot_nn(left, right):
    return jnp.dot(left, right, preferred_element_type=F32)


def attention_kernel(
    length_ref,
    core_ref,
    tokens_ref,
    own_ref,
    other_ref,
    cos_ref,
    sin_ref,
    gain_in_ref,
    gain_mid_ref,
    middle_ref,
    normed_ref,
    cache_ref,
    qkv,
    attended,
    mid,
):
    length = length_ref[0]
    core = core_ref[0]
    halves = ((own_ref, core), (other_ref, 1 - core))
    stream = tokens_ref[...].astype(F32)
    square = jnp.mean(stream * stream, axis=-1, keepdims=True)
    normed = (stream * lax.rsqrt(square + 1e-05) * gain_in_ref[...]).astype(BF16)
    low, high = normed[:, :KHALF], normed[:, KHALF:]
    for weights, half in halves:
        for s in range(8):
            rows = dot_nt(weights[s, OW : OW + QW, :], low) + dot_nt(
                weights[8 + s, OW : OW + QW, :], high
            )
            start = pl.multiple_of((2 * s + half) * QW, 8)
            qkv[pl.ds(start, QW), :] = rows.astype(BF16).astype(F32)
    cosine = cos_ref[...]
    sine = sin_ref[...]

    def rotate(start):
        first = qkv[start : start + 32, :]
        second = qkv[start + 32 : start + 64, :]
        return jnp.concatenate(
            [first * cosine - second * sine, second * cosine + first * sine], axis=0
        )

    key_at = lax.broadcasted_iota(jnp.int32, (LMAX, LMAX), 0)
    query_at = lax.broadcasted_iota(jnp.int32, (LMAX, LMAX), 1)
    allowed = (key_at <= query_at) & (key_at < length)
    allowed = jnp.concatenate([allowed.astype(F32)] * 4, axis=1) > 0.5
    for g in range(KEY_VALUE_HEADS):
        key_start = (QUERY_HEADS + g) * HEAD_SIZE
        value_start = (QUERY_HEADS + KEY_VALUE_HEADS + g) * HEAD_SIZE
        keys = rotate(key_start).astype(BF16).astype(F32)
        qkv[key_start : key_start + HEAD_SIZE, :] = keys
        keys = keys.T.astype(BF16)
        values = qkv[value_start : value_start + HEAD_SIZE, :].astype(BF16)
        queries = jnp.concatenate(
            [rotate((4 * g + h) * HEAD_SIZE).astype(BF16) for h in range(4)], axis=1
        )
        scores = dot_nn(keys, queries) * HEAD_SIZE ** (-0.5)
        scores = jnp.where(allowed, scores, -1e30)
        weights = jnp.exp(scores - jnp.max(scores, axis=0, keepdims=True))
        probability = (weights / jnp.sum(weights, axis=0, keepdims=True)).astype(BF16)
        out = dot_nn(values, probability).astype(BF16)
        for h in range(4):
            row = (4 * g + h) * HEAD_SIZE
            attended[row : row + HEAD_SIZE, :] = out[:, h * LMAX : (h + 1) * LMAX]
    live = (lax.broadcasted_iota(jnp.int32, (LMAX, LMAX), 0) < length).astype(F32)
    for j in range(5):
        row = QUERY_HEADS * HEAD_SIZE + j * LMAX
        block = qkv[row : row + LMAX, :].T
        cache_ref[:, j * LMAX : (j + 1) * LMAX] = (live * block).astype(BF16)
    low, high = attended[:KHALF, :], attended[KHALF:, :]
    for weights, half in halves:
        for s in range(8):
            rows = dot_nn(weights[s, :OW, :], low) + dot_nn(weights[8 + s, :OW, :], high)
            start = pl.multiple_of((2 * s + half) * OW, 8)
            mid[pl.ds(start, OW), :] = rows
    total = jnp.zeros((1, LMAX), F32)
    for j in range(10):
        cols = slice(j * LMAX, (j + 1) * LMAX)
        block = mid[cols, :] + tokens_ref[:, cols].astype(F32).T
        mid[cols, :] = block
        middle_ref[:, cols] = block.T
        total = total + jnp.sum(block * block, axis=0, keepdims=True)
    scale = lax.rsqrt(total * (1.0 / D) + 1e-05)
    for j in range(16):
        for lo in range(2):
            start = lo * KHALF + j * 40
            block = mid[start : start + 40, :] * scale * gain_mid_ref[start : start + 40, :]
            qkv[j * 80 + lo * 40 : j * 80 + lo * 40 + 40, :] = block
    for j in range(10):
        cols = slice(j * LMAX, (j + 1) * LMAX)
        normed_ref[:, cols] = qkv[cols, :].T.astype(BF16)


def attention(length, core, tokens, own, other, gain_in, gain_mid):
    cosine, sine = tables()
    vmem = pl.BlockSpec(memory_space=pltpu.VMEM)
    smem = pl.BlockSpec(memory_space=pltpu.SMEM)
    return pl.pallas_call(
        attention_kernel,
        out_shape=(
            jax.ShapeDtypeStruct((LMAX, D), F32),
            jax.ShapeDtypeStruct((LMAX, D), BF16),
            jax.ShapeDtypeStruct((LMAX, 640), BF16),
        ),
        in_specs=[smem, smem] + [vmem] * 7,
        out_specs=(vmem, vmem, vmem),
        scratch_shapes=[
            pltpu.VMEM((1920, LMAX), F32),
            pltpu.VMEM((D, LMAX), BF16),
            pltpu.VMEM((D, LMAX), F32),
        ],
        compiler_params=pltpu.CompilerParams(vmem_limit_bytes=32 << 20),
        cost_estimate=pl.CostEstimate(
            flops=1200000000, bytes_accessed=10000000, transcendentals=400000
        ),
        name="attention",
    )(
        length,
        core,
        tokens,
        own,
        other,
        jnp.asarray(cosine),
        jnp.asarray(sine),
        gain_in[None, :],
        gain_mid[:, None],
    )


def spread(block, axes, count):
    copies = jnp.broadcast_to(block[None], (count,) + block.shape)
    return lax.all_to_all(copies, axes, 0, 0, tiled=False)


def after(value, *others):
    return lax.optimization_barrier((value,) + others)[0]


SWAP = [(0, 1), (1, 0)]


def shards(
    prompts, lengths, qkv_master, out_master, gate_up_master, down_weight, attn_gain, mlp_gain
):
    core = lax.axis_index("core")
    x_hi = lax.axis_index("x_hi")
    tokens = prompts[0]
    gate_up = gate_up_master.astype(BF16).reshape(20, 2 * UNITS)
    near = spread(gate_up, ("x_lo", "core", "x_hi"), 8).reshape(4, 2, 20, 2 * UNITS)
    near = lax.dynamic_index_in_dim(near, core, axis=1, keepdims=False).reshape(80, 2 * UNITS)
    gate_up_own = lax.all_gather(near, "z", axis=0, tiled=True)
    down_other = lax.ppermute(down_weight, "x_hi", SWAP)
    merged = jnp.concatenate([out_master, qkv_master], axis=1).astype(BF16)
    merged = lax.all_gather(merged, "core", axis=0, tiled=True)
    part = jnp.concatenate(
        [
            lax.dynamic_slice_in_dim(merged[:, :160], core * OW, OW, axis=1),
            lax.dynamic_slice_in_dim(merged[:, 160:], core * QW, QW, axis=1),
        ],
        axis=1,
    )
    part = after(part, near)
    part = spread(part, "z", 16).reshape(KHALF, OW + QW).T
    own = spread(part, ("x_lo", "y", "x_hi"), 16)
    other = lax.ppermute(own, "core", SWAP)
    gate_up_other = lax.ppermute(after(gate_up_own, own), "core", SWAP)
    middle, normed_mid, cache = attention(
        lengths, core.astype(jnp.int32)[None], tokens, own, other, attn_gain, mlp_gain
    )
    gathered = spread(normed_mid, "y", 4).reshape(4 * LMAX, D)
    same = core == x_hi
    down_first = jnp.where(same, down_weight, down_other)
    down_second = jnp.where(same, down_other, down_weight)

    def units_block(gate_up_rows, down_rows):
        gate_up = jnp.dot(gathered, gate_up_rows, preferred_element_type=F32)
        hidden_units = (jax.nn.silu(gate_up[:, :UNITS]) * gate_up[:, UNITS:]).astype(BF16)
        return jnp.dot(hidden_units, down_rows, preferred_element_type=F32).astype(BF16)

    partial = units_block(gate_up_own, down_first).astype(F32) + units_block(
        gate_up_other, down_second
    ).astype(F32)
    partial = partial.astype(BF16).reshape(4, LMAX, D)
    partial = lax.all_to_all(partial, "y", 0, 0, tiled=False)
    feed_out = jnp.sum(partial.astype(F32), axis=0)
    live_rows = (jnp.arange(LMAX) < lengths[0]).astype(F32)[:, None]
    hidden = (live_rows * (middle + feed_out)).astype(BF16)
    return (hidden[None], cache[None])


def solution(mesh):
    fine = Mesh(mesh.devices.reshape(SIZES), AXES)
    group = ("x_lo", "z", "core")
    shard = ("y", "x_hi")
    in_specs = (
        P(group + shard, None, None),
        P(group + shard),
        P(group, shard),
        P(group, shard),
        P(group, None, shard),
        P(shard, None),
        P(),
        P(),
    )
    out_specs = (P(group + shard, None, None), P(group + shard, None, None))
    return jax.shard_map(shards, mesh=fine, in_specs=in_specs, out_specs=out_specs, check_vma=False)
```

```python
import jax
import jax.numpy as jnp
import numpy as np
from jax import lax
from jax.experimental import pallas as pl
from jax.experimental.pallas import tpu as pltpu
from jax.sharding import Mesh, PartitionSpec as P

QUERY_HEADS = 20
KEY_VALUE_HEADS = 5
HEAD_SIZE = 64
D = 1280
LMAX = 128
QW = 120
OW = 80
KHALF = 640
UNITS = 448
F32 = jnp.float32
BF16 = jnp.bfloat16

AXES = ("x_lo", "z", "core", "y", "x_hi")
SIZES = (2, 16, 2, 4, 2)


def tables():
    half_dim = HEAD_SIZE // 2
    frequency = np.float32(10000.0) ** (
        -(np.arange(half_dim).astype(np.float32) * np.float32(2.0) / np.float32(HEAD_SIZE))
    )
    angles = frequency.astype(np.float32)[:, None] * np.arange(LMAX).astype(np.float32)[None, :]
    return np.cos(angles).astype(np.float32), np.sin(angles).astype(np.float32)


def dot_nt(left, right):
    return lax.dot_general(left, right, (((1,), (1,)), ((), ())), preferred_element_type=F32)


def dot_nn(left, right):
    return jnp.dot(left, right, preferred_element_type=F32)


def attention_kernel(
    length_ref,
    core_ref,
    tokens_ref,
    own_ref,
    other_ref,
    cos_ref,
    sin_ref,
    gain_ref,
    attended_ref,
    cache_ref,
    qkv,
):
    length = length_ref[0]
    core = core_ref[0]
    stream = tokens_ref[...].astype(F32)
    square = jnp.mean(stream * stream, axis=-1, keepdims=True)
    normed = (stream * lax.rsqrt(square + 1e-05) * gain_ref[...]).astype(BF16)
    low, high = normed[:, :KHALF], normed[:, KHALF:]
    for weights, half in ((own_ref, core), (other_ref, 1 - core)):
        for s in range(8):
            rows = dot_nt(weights[s], low) + dot_nt(weights[8 + s], high)
            start = pl.multiple_of((2 * s + half) * QW, 8)
            qkv[pl.ds(start, QW), :] = rows.astype(BF16).astype(F32)
    cosine = cos_ref[...]
    sine = sin_ref[...]

    def rotate(start):
        first = qkv[start : start + 32, :]
        second = qkv[start + 32 : start + 64, :]
        return jnp.concatenate(
            [first * cosine - second * sine, second * cosine + first * sine], axis=0
        )

    key_at = lax.broadcasted_iota(jnp.int32, (LMAX, LMAX), 0)
    query_at = lax.broadcasted_iota(jnp.int32, (LMAX, LMAX), 1)
    allowed = (key_at <= query_at) & (key_at < length)
    allowed = jnp.concatenate([allowed.astype(F32)] * 4, axis=1) > 0.5
    for g in range(KEY_VALUE_HEADS):
        key_start = (QUERY_HEADS + g) * HEAD_SIZE
        value_start = (QUERY_HEADS + KEY_VALUE_HEADS + g) * HEAD_SIZE
        keys = rotate(key_start).astype(BF16).astype(F32)
        qkv[key_start : key_start + HEAD_SIZE, :] = keys
        keys = keys.T.astype(BF16)
        values = qkv[value_start : value_start + HEAD_SIZE, :].astype(BF16)
        queries = jnp.concatenate(
            [rotate((4 * g + h) * HEAD_SIZE).astype(BF16) for h in range(4)], axis=1
        )
        scores = dot_nn(keys, queries) * HEAD_SIZE ** (-0.5)
        scores = jnp.where(allowed, scores, -1e30)
        weights = jnp.exp(scores - jnp.max(scores, axis=0, keepdims=True))
        probability = (weights / jnp.sum(weights, axis=0, keepdims=True)).astype(BF16)
        out = dot_nn(values, probability).astype(BF16)
        for h in range(4):
            row = (4 * g + h) * HEAD_SIZE
            attended_ref[row : row + HEAD_SIZE, :] = out[:, h * LMAX : (h + 1) * LMAX]
    live = (lax.broadcasted_iota(jnp.int32, (LMAX, LMAX), 0) < length).astype(F32)
    for j in range(5):
        row = QUERY_HEADS * HEAD_SIZE + j * LMAX
        block = qkv[row : row + LMAX, :].T
        cache_ref[:, j * LMAX : (j + 1) * LMAX] = (live * block).astype(BF16)


def middle_kernel(
    core_ref,
    tokens_ref,
    attended_ref,
    own_ref,
    other_ref,
    gain_ref,
    middle_ref,
    normed_ref,
    mid,
    moved,
):
    core = core_ref[0]
    low, high = attended_ref[:KHALF, :], attended_ref[KHALF:, :]
    for weights, half in ((own_ref, core), (other_ref, 1 - core)):
        for s in range(8):
            rows = dot_nn(weights[s], low) + dot_nn(weights[8 + s], high)
            start = pl.multiple_of((2 * s + half) * OW, 8)
            mid[pl.ds(start, OW), :] = rows
    total = jnp.zeros((1, LMAX), F32)
    for j in range(10):
        cols = slice(j * LMAX, (j + 1) * LMAX)
        block = mid[cols, :] + tokens_ref[:, cols].astype(F32).T
        mid[cols, :] = block
        middle_ref[:, cols] = block.T
        total = total + jnp.sum(block * block, axis=0, keepdims=True)
    scale = lax.rsqrt(total * (1.0 / D) + 1e-05)
    for j in range(16):
        for lo in range(2):
            start = lo * KHALF + j * 40
            block = mid[start : start + 40, :] * scale * gain_ref[start : start + 40, :]
            moved[j * 80 + lo * 40 : j * 80 + lo * 40 + 40, :] = block
    for j in range(10):
        cols = slice(j * LMAX, (j + 1) * LMAX)
        normed_ref[:, cols] = moved[cols, :].T.astype(BF16)


VMEM = pl.BlockSpec(memory_space=pltpu.VMEM)
SMEM = pl.BlockSpec(memory_space=pltpu.SMEM)


def attention(length, core, tokens, own, other, gain):
    cosine, sine = tables()
    return pl.pallas_call(
        attention_kernel,
        out_shape=(
            jax.ShapeDtypeStruct((D, LMAX), BF16),
            jax.ShapeDtypeStruct((LMAX, 640), BF16),
        ),
        in_specs=[SMEM, SMEM] + [VMEM] * 6,
        out_specs=(VMEM, VMEM),
        scratch_shapes=[pltpu.VMEM((1920, LMAX), F32)],
        compiler_params=pltpu.CompilerParams(vmem_limit_bytes=32 << 20),
        cost_estimate=pl.CostEstimate(
            flops=800000000, bytes_accessed=6000000, transcendentals=400000
        ),
        name="attention",
    )(
        length, core, tokens, own, other, jnp.asarray(cosine), jnp.asarray(sine), gain[None, :]
    )


def middle_rows(core, tokens, attended, own, other, gain):
    return pl.pallas_call(
        middle_kernel,
        out_shape=(
            jax.ShapeDtypeStruct((LMAX, D), F32),
            jax.ShapeDtypeStruct((LMAX, D), BF16),
        ),
        in_specs=[SMEM] + [VMEM] * 5,
        out_specs=(VMEM, VMEM),
        scratch_shapes=[pltpu.VMEM((D, LMAX), F32), pltpu.VMEM((D, LMAX), F32)],
        compiler_params=pltpu.CompilerParams(vmem_limit_bytes=32 << 20),
        cost_estimate=pl.CostEstimate(
            flops=420000000, bytes_accessed=4000000, transcendentals=1000
        ),
        name="middle",
    )(core, tokens, attended, own, other, gain[:, None])


def spread(block, axes, count):
    copies = jnp.broadcast_to(block[None], (count,) + block.shape)
    return lax.all_to_all(copies, axes, 0, 0, tiled=False)


def after(value, *others):
    return lax.optimization_barrier((value,) + others)[0]


SWAP = [(0, 1), (1, 0)]


def shards(
    prompts, lengths, qkv_master, out_master, gate_up_master, down_weight, attn_gain, mlp_gain
):
    core = lax.axis_index("core")
    x_hi = lax.axis_index("x_hi")
    core_at = core.astype(jnp.int32)[None]
    tokens = prompts[0]
    gate_up = gate_up_master.astype(BF16).reshape(20, 2 * UNITS)
    near = spread(gate_up, ("x_lo", "core", "x_hi"), 8).reshape(4, 2, 20, 2 * UNITS)
    near = lax.dynamic_index_in_dim(near, core, axis=1, keepdims=False).reshape(80, 2 * UNITS)
    gate_up_own = lax.all_gather(near, "z", axis=0, tiled=True)
    merged = jnp.concatenate([out_master, qkv_master], axis=1).astype(BF16)
    merged = lax.all_gather(merged, "core", axis=0, tiled=True)
    part = jnp.concatenate(
        [
            lax.dynamic_slice_in_dim(merged[:, :160], core * OW, OW, axis=1),
            lax.dynamic_slice_in_dim(merged[:, 160:], core * QW, QW, axis=1),
        ],
        axis=1,
    )
    part = spread(after(part, near), "z", 16).reshape(KHALF, OW + QW).T
    down_other = lax.ppermute(down_weight, "x_hi", SWAP)
    qkv_own = spread(after(part[OW:], down_other), ("x_lo", "y", "x_hi"), 16)
    out_own = spread(after(part[:OW], qkv_own), ("x_lo", "y", "x_hi"), 16)
    qkv_other = lax.ppermute(qkv_own, "core", SWAP)
    attended, cache = attention(lengths, core_at, tokens, qkv_own, qkv_other, attn_gain)
    out_own = after(out_own, attended)
    out_other = lax.ppermute(out_own, "core", SWAP)
    middle, normed_mid = middle_rows(core_at, tokens, attended, out_own, out_other, mlp_gain)
    gate_up_other = lax.ppermute(after(gate_up_own, normed_mid), "core", SWAP)
    gathered = spread(normed_mid, "y", 4).reshape(4 * LMAX, D)
    same = core == x_hi
    down_first = jnp.where(same, down_weight, down_other)
    down_second = jnp.where(same, down_other, down_weight)

    def units_block(gate_up_rows, down_rows):
        gate_up = jnp.dot(gathered, gate_up_rows, preferred_element_type=F32)
        hidden_units = (jax.nn.silu(gate_up[:, :UNITS]) * gate_up[:, UNITS:]).astype(BF16)
        return jnp.dot(hidden_units, down_rows, preferred_element_type=F32).astype(BF16)

    partial = units_block(gate_up_own, down_first).astype(F32) + units_block(
        gate_up_other, down_second
    ).astype(F32)
    partial = partial.astype(BF16).reshape(4, LMAX, D)
    partial = lax.all_to_all(partial, "y", 0, 0, tiled=False)
    feed_out = jnp.sum(partial.astype(F32), axis=0)
    live_rows = (jnp.arange(LMAX) < lengths[0]).astype(F32)[:, None]
    hidden = (live_rows * (middle + feed_out)).astype(BF16)
    return (hidden[None], cache[None])


def solution(mesh):
    fine = Mesh(mesh.devices.reshape(SIZES), AXES)
    group = ("x_lo", "z", "core")
    shard = ("y", "x_hi")
    in_specs = (
        P(group + shard, None, None),
        P(group + shard),
        P(group, shard),
        P(group, shard),
        P(group, None, shard),
        P(shard, None),
        P(),
        P(),
    )
    out_specs = (P(group + shard, None, None), P(group + shard, None, None))
    return jax.shard_map(shards, mesh=fine, in_specs=in_specs, out_specs=out_specs, check_vma=False)
```

```python
import jax
import jax.numpy as jnp
import numpy as np
from jax import lax
from jax.experimental import pallas as pl
from jax.experimental.pallas import tpu as pltpu
from jax.sharding import Mesh, PartitionSpec as P

QUERY_HEADS = 20
KEY_VALUE_HEADS = 5
HEAD_SIZE = 64
D = 1280
LMAX = 128
QW = 120
OW = 80
KHALF = 640
UNITS = 448
WIDE = 384
F32 = jnp.float32
BF16 = jnp.bfloat16

AXES = ("x_lo", "z", "core", "y", "x_hi")
SIZES = (2, 16, 2, 4, 2)


def tables():
    half_dim = HEAD_SIZE // 2
    frequency = np.float32(10000.0) ** (
        -(np.arange(half_dim).astype(np.float32) * np.float32(2.0) / np.float32(HEAD_SIZE))
    )
    angles = frequency.astype(np.float32)[:, None] * np.arange(LMAX).astype(np.float32)[None, :]
    return np.cos(angles).astype(np.float32), np.sin(angles).astype(np.float32)


def dot_nt(left, right):
    return lax.dot_general(left, right, (((1,), (1,)), ((), ())), preferred_element_type=F32)


def dot_nn(left, right):
    return jnp.dot(left, right, preferred_element_type=F32)


def attention_kernel(
    length_ref,
    core_ref,
    tokens_ref,
    own_ref,
    other_ref,
    cos_ref,
    sin_ref,
    gain_ref,
    attended_ref,
    cache_ref,
    qkv,
):
    length = length_ref[0]
    core = core_ref[0]
    stream = tokens_ref[...].astype(F32)
    square = jnp.mean(stream * stream, axis=-1, keepdims=True)
    normed = (stream * lax.rsqrt(square + 1e-05) * gain_ref[...]).astype(BF16)
    low, high = normed[:, :KHALF], normed[:, KHALF:]
    for weights, half in ((own_ref, core), (other_ref, 1 - core)):
        for s in range(8):
            rows = dot_nt(weights[s], low) + dot_nt(weights[8 + s], high)
            start = pl.multiple_of((2 * s + half) * QW, 8)
            qkv[pl.ds(start, QW), :] = rows.astype(BF16).astype(F32)
    cosine = cos_ref[...]
    sine = sin_ref[...]

    def rotate(start):
        first = qkv[start : start + 32, :]
        second = qkv[start + 32 : start + 64, :]
        return jnp.concatenate(
            [first * cosine - second * sine, second * cosine + first * sine], axis=0
        )

    key_at = lax.broadcasted_iota(jnp.int32, (LMAX, LMAX), 0)
    query_at = lax.broadcasted_iota(jnp.int32, (LMAX, LMAX), 1)
    allowed = (key_at <= query_at) & (key_at < length)
    allowed = jnp.concatenate([allowed.astype(F32)] * 4, axis=1) > 0.5
    for g in range(KEY_VALUE_HEADS):
        key_start = (QUERY_HEADS + g) * HEAD_SIZE
        value_start = (QUERY_HEADS + KEY_VALUE_HEADS + g) * HEAD_SIZE
        keys = rotate(key_start).astype(BF16).astype(F32)
        qkv[key_start : key_start + HEAD_SIZE, :] = keys
        keys = keys.T.astype(BF16)
        values = qkv[value_start : value_start + HEAD_SIZE, :].astype(BF16)
        queries = jnp.concatenate(
            [rotate((4 * g + h) * HEAD_SIZE).astype(BF16) for h in range(4)], axis=1
        )
        scores = dot_nn(keys, queries) * HEAD_SIZE ** (-0.5)
        scores = jnp.where(allowed, scores, -1e30)
        weights = jnp.exp(scores - jnp.max(scores, axis=0, keepdims=True))
        probability = (weights / jnp.sum(weights, axis=0, keepdims=True)).astype(BF16)
        out = dot_nn(values, probability).astype(BF16)
        for h in range(4):
            row = (4 * g + h) * HEAD_SIZE
            attended_ref[row : row + HEAD_SIZE, :] = out[:, h * LMAX : (h + 1) * LMAX]
    live = (lax.broadcasted_iota(jnp.int32, (LMAX, LMAX), 0) < length).astype(F32)
    for j in range(5):
        row = QUERY_HEADS * HEAD_SIZE + j * LMAX
        block = qkv[row : row + LMAX, :].T
        cache_ref[:, j * LMAX : (j + 1) * LMAX] = (live * block).astype(BF16)


def middle_kernel(
    core_ref,
    tokens_ref,
    attended_ref,
    own_ref,
    other_ref,
    gain_ref,
    middle_ref,
    normed_ref,
    mid,
    moved,
):
    core = core_ref[0]
    low, high = attended_ref[:KHALF, :], attended_ref[KHALF:, :]
    for weights, half in ((own_ref, core), (other_ref, 1 - core)):
        for s in range(8):
            rows = dot_nn(weights[s], low) + dot_nn(weights[8 + s], high)
            start = pl.multiple_of((2 * s + half) * OW, 8)
            mid[pl.ds(start, OW), :] = rows
    total = jnp.zeros((1, LMAX), F32)
    for j in range(10):
        cols = slice(j * LMAX, (j + 1) * LMAX)
        block = mid[cols, :] + tokens_ref[:, cols].astype(F32).T
        mid[cols, :] = block
        middle_ref[:, cols] = block.T
        total = total + jnp.sum(block * block, axis=0, keepdims=True)
    scale = lax.rsqrt(total * (1.0 / D) + 1e-05)
    for j in range(16):
        for lo in range(2):
            start = lo * KHALF + j * 40
            block = mid[start : start + 40, :] * scale * gain_ref[start : start + 40, :]
            moved[j * 80 + lo * 40 : j * 80 + lo * 40 + 40, :] = block
    for j in range(10):
        cols = slice(j * LMAX, (j + 1) * LMAX)
        block = moved[cols, :].T.astype(BF16)
        for copy in range(4):
            normed_ref[copy, :, cols] = block


def hidden_kernel(
    same_ref, tokens_ref, first_ref, second_ref, down_own_ref, down_other_ref, out_ref
):
    def block(tokens, gate_up_ref, down_ref):
        gate_up = dot_nn(tokens, gate_up_ref[...])
        gate, up = gate_up[:, :WIDE], gate_up[:, WIDE : 2 * WIDE]
        units = (gate / (1.0 + jnp.exp(-gate)) * up).astype(BF16)
        gate = gate_up[:, 2 * WIDE :]
        up = pltpu.roll(gate, 64, 1)
        rest = (gate / (1.0 + jnp.exp(-gate)) * up).astype(BF16)[:, :64]
        total = dot_nn(units, down_ref[:WIDE, :]) + dot_nn(rest, down_ref[WIDE:, :])
        return total.astype(BF16).astype(F32)

    def run(down_first_ref, down_second_ref):
        for prompt in range(4):
            tokens = tokens_ref[prompt]
            total = block(tokens, first_ref, down_first_ref)
            total = total + block(tokens, second_ref, down_second_ref)
            out_ref[prompt] = total.astype(BF16)

    @pl.when(same_ref[0] == 1)
    def _():
        run(down_own_ref, down_other_ref)

    @pl.when(same_ref[0] == 0)
    def _():
        run(down_other_ref, down_own_ref)


def result_kernel(length_ref, middle_ref, parts_ref, out_ref):
    feed_out = parts_ref[0].astype(F32)
    for j in range(1, 4):
        feed_out = feed_out + parts_ref[j].astype(F32)
    live = lax.broadcasted_iota(jnp.int32, (LMAX, D), 0) < length_ref[0]
    out_ref[...] = jnp.where(live, middle_ref[...] + feed_out, 0.0).astype(BF16)


VMEM = pl.BlockSpec(memory_space=pltpu.VMEM)
SMEM = pl.BlockSpec(memory_space=pltpu.SMEM)


def attention(length, core, tokens, own, other, gain):
    cosine, sine = tables()
    return pl.pallas_call(
        attention_kernel,
        out_shape=(
            jax.ShapeDtypeStruct((D, LMAX), BF16),
            jax.ShapeDtypeStruct((LMAX, 640), BF16),
        ),
        in_specs=[SMEM, SMEM] + [VMEM] * 6,
        out_specs=(VMEM, VMEM),
        scratch_shapes=[pltpu.VMEM((1920, LMAX), F32)],
        compiler_params=pltpu.CompilerParams(vmem_limit_bytes=32 << 20),
        cost_estimate=pl.CostEstimate(
            flops=800000000, bytes_accessed=6000000, transcendentals=400000
        ),
        name="attention",
    )(
        length, core, tokens, own, other, jnp.asarray(cosine), jnp.asarray(sine), gain[None, :]
    )


def middle_rows(core, tokens, attended, own, other, gain):
    return pl.pallas_call(
        middle_kernel,
        out_shape=(
            jax.ShapeDtypeStruct((LMAX, D), F32),
            jax.ShapeDtypeStruct((4, LMAX, D), BF16),
        ),
        in_specs=[SMEM] + [VMEM] * 5,
        out_specs=(VMEM, VMEM),
        scratch_shapes=[pltpu.VMEM((D, LMAX), F32), pltpu.VMEM((D, LMAX), F32)],
        compiler_params=pltpu.CompilerParams(vmem_limit_bytes=32 << 20),
        cost_estimate=pl.CostEstimate(
            flops=420000000, bytes_accessed=4000000, transcendentals=1000
        ),
        name="middle",
    )(core, tokens, attended, own, other, gain[:, None])


def hidden_rows(same, tokens, first, second, down_own, down_other):
    return pl.pallas_call(
        hidden_kernel,
        out_shape=jax.ShapeDtypeStruct((4, LMAX, D), BF16),
        in_specs=[SMEM] + [VMEM] * 5,
        out_specs=VMEM,
        compiler_params=pltpu.CompilerParams(vmem_limit_bytes=32 << 20),
        cost_estimate=pl.CostEstimate(
            flops=3500000000, bytes_accessed=9500000, transcendentals=500000
        ),
        name="hidden",
    )(same, tokens, first, second, down_own, down_other)


def result(length, middle, parts):
    return pl.pallas_call(
        result_kernel,
        out_shape=jax.ShapeDtypeStruct((LMAX, D), BF16),
        in_specs=[SMEM] + [VMEM] * 2,
        out_specs=VMEM,
        cost_estimate=pl.CostEstimate(flops=1000000, bytes_accessed=2300000, transcendentals=0),
        name="result",
    )(length, middle, parts)


def turn(same_x):
    pairs = []
    for lo in range(2):
        for core in range(2):
            for hi in range(2):
                to_lo = lo if same_x else 1 - lo
                pairs.append((lo * 4 + core * 2 + hi, to_lo * 4 + hi * 2 + core))
    return pairs


def spread(block, axes, count):
    copies = jnp.broadcast_to(block[None], (count,) + block.shape)
    return lax.all_to_all(copies, axes, 0, 0, tiled=False)


def after(value, *others):
    return lax.optimization_barrier((value,) + others)[0]


SWAP = [(0, 1), (1, 0)]


def shards(
    prompts, lengths, qkv_master, out_master, gate_up_master, down_weight, attn_gain, mlp_gain
):
    core = lax.axis_index("core").astype(jnp.int32)
    x_hi = lax.axis_index("x_hi").astype(jnp.int32)
    x_lo = lax.axis_index("x_lo")
    core_at = core[None]
    same = (core == x_hi).astype(jnp.int32)[None]
    tokens = prompts[0]
    gate_up = gate_up_master.astype(BF16)
    merged = jnp.concatenate(
        [
            out_master.astype(BF16),
            qkv_master.astype(BF16),
            gate_up[:, 0, :WIDE],
            gate_up[:, 1, :WIDE],
            gate_up[:, 0, WIDE:],
            gate_up[:, 1, WIDE:],
        ],
        axis=1,
    )
    merged = lax.all_gather(merged, "core", axis=0, tiled=True)
    part = jnp.concatenate(
        [
            lax.dynamic_slice_in_dim(merged[:, 160:400], core * QW, QW, axis=1),
            jnp.zeros((40, 128 - QW), BF16),
            lax.dynamic_slice_in_dim(merged[:, :160], core * OW, OW, axis=1),
            jnp.zeros((40, 128 - OW), BF16),
        ],
        axis=1,
    )
    part = spread(part, "z", 16).reshape(KHALF, 256)
    rows = merged[:, 400:]
    along = ("x_lo", "core", "x_hi")
    near = lax.ppermute(rows, along, turn(True))
    far = lax.ppermute(rows, along, turn(False))
    near = jnp.where(
        x_lo == 0, jnp.concatenate([near, far], axis=0), jnp.concatenate([far, near], axis=0)
    )
    gate_up_own = lax.all_gather(near, "z", axis=0, tiled=True)
    down_other = lax.ppermute(after(down_weight, merged), "x_hi", SWAP)
    part_qkv = after(part[:, :QW].T, near, down_other)
    qkv_own = spread(part_qkv, ("x_lo", "y", "x_hi"), 16)
    part_out = after(part[:, 128 : 128 + OW].T, qkv_own)
    out_own = spread(part_out, ("x_lo", "y", "x_hi"), 16)
    qkv_other = lax.ppermute(qkv_own, "core", SWAP)
    attended, cache = attention(lengths, core_at, tokens, qkv_own, qkv_other, attn_gain)
    out_own = after(out_own, attended)
    out_other = lax.ppermute(out_own, "core", SWAP)
    middle, normed_mid = middle_rows(core_at, tokens, attended, out_own, out_other, mlp_gain)
    gate_up_other = lax.ppermute(after(gate_up_own, middle), "core", SWAP)
    normed_mid = after(normed_mid, same)
    gathered = lax.all_to_all(normed_mid, "y", 0, 0, tiled=False)
    partial = hidden_rows(same, gathered, gate_up_own, gate_up_other, down_weight, down_other)
    parts = lax.all_to_all(partial, "y", 0, 0, tiled=False)
    hidden = result(lengths, middle, parts)
    return (hidden[None], cache[None])


def solution(mesh):
    fine = Mesh(mesh.devices.reshape(SIZES), AXES)
    group = ("x_lo", "z", "core")
    shard = ("y", "x_hi")
    in_specs = (
        P(group + shard, None, None),
        P(group + shard),
        P(group, shard),
        P(group, shard),
        P(group, None, shard),
        P(shard, None),
        P(),
        P(),
    )
    out_specs = (P(group + shard, None, None), P(group + shard, None, None))
    return jax.shard_map(shards, mesh=fine, in_specs=in_specs, out_specs=out_specs, check_vma=False)
```

```python
import jax
import jax.numpy as jnp
import numpy as np
from jax import lax
from jax.experimental import pallas as pl
from jax.experimental.pallas import tpu as pltpu
from jax.sharding import Mesh, PartitionSpec as P

QUERY_HEADS = 20
KEY_VALUE_HEADS = 5
HEAD_SIZE = 64
D = 1280
LMAX = 128
QW = 120
OW = 80
KHALF = 640
UNITS = 448
WIDE = 384
F32 = jnp.float32
BF16 = jnp.bfloat16

AXES = ("x_lo", "z", "core", "y", "x_hi")
SIZES = (2, 16, 2, 4, 2)


def tables():
    half_dim = HEAD_SIZE // 2
    frequency = np.float32(10000.0) ** (
        -(np.arange(half_dim).astype(np.float32) * np.float32(2.0) / np.float32(HEAD_SIZE))
    )
    angles = frequency.astype(np.float32)[:, None] * np.arange(LMAX).astype(np.float32)[None, :]
    return np.cos(angles).astype(np.float32), np.sin(angles).astype(np.float32)


def dot_nt(left, right):
    return lax.dot_general(left, right, (((1,), (1,)), ((), ())), preferred_element_type=F32)


def dot_nn(left, right):
    return jnp.dot(left, right, preferred_element_type=F32)


def attention_kernel(
    length_ref,
    core_ref,
    tokens_ref,
    own_ref,
    other_ref,
    cos_ref,
    sin_ref,
    gain_ref,
    attended_ref,
    cache_ref,
    qkv,
):
    length = length_ref[0]
    core = core_ref[0]
    stream = tokens_ref[...].astype(F32)
    square = jnp.mean(stream * stream, axis=-1, keepdims=True)
    normed = (stream * lax.rsqrt(square + 1e-05) * gain_ref[...]).astype(BF16)
    low, high = normed[:, :KHALF], normed[:, KHALF:]
    for weights, half in ((own_ref, core), (other_ref, 1 - core)):
        for s in range(8):
            rows = dot_nt(weights[s], low) + dot_nt(weights[8 + s], high)
            start = pl.multiple_of((2 * s + half) * QW, 8)
            qkv[pl.ds(start, QW), :] = rows.astype(BF16).astype(F32)
    cosine = cos_ref[...]
    sine = sin_ref[...]

    def rotate(start):
        first = qkv[start : start + 32, :]
        second = qkv[start + 32 : start + 64, :]
        return jnp.concatenate(
            [first * cosine - second * sine, second * cosine + first * sine], axis=0
        )

    key_at = lax.broadcasted_iota(jnp.int32, (LMAX, LMAX), 0)
    query_at = lax.broadcasted_iota(jnp.int32, (LMAX, LMAX), 1)
    allowed = (key_at <= query_at) & (key_at < length)
    allowed = jnp.concatenate([allowed.astype(F32)] * 4, axis=1) > 0.5
    for g in range(KEY_VALUE_HEADS):
        key_start = (QUERY_HEADS + g) * HEAD_SIZE
        value_start = (QUERY_HEADS + KEY_VALUE_HEADS + g) * HEAD_SIZE
        keys = rotate(key_start).astype(BF16).astype(F32)
        qkv[key_start : key_start + HEAD_SIZE, :] = keys
        keys = keys.T.astype(BF16)
        values = qkv[value_start : value_start + HEAD_SIZE, :].astype(BF16)
        queries = jnp.concatenate(
            [rotate((4 * g + h) * HEAD_SIZE).astype(BF16) for h in range(4)], axis=1
        )
        scores = dot_nn(keys, queries) * HEAD_SIZE ** (-0.5)
        scores = jnp.where(allowed, scores, -1e30)
        weights = jnp.exp(scores - jnp.max(scores, axis=0, keepdims=True))
        probability = (weights / jnp.sum(weights, axis=0, keepdims=True)).astype(BF16)
        out = dot_nn(values, probability).astype(BF16)
        for h in range(4):
            row = (4 * g + h) * HEAD_SIZE
            attended_ref[row : row + HEAD_SIZE, :] = out[:, h * LMAX : (h + 1) * LMAX]
    live = (lax.broadcasted_iota(jnp.int32, (LMAX, LMAX), 0) < length).astype(F32)
    for j in range(5):
        row = QUERY_HEADS * HEAD_SIZE + j * LMAX
        block = qkv[row : row + LMAX, :].T
        cache_ref[:, j * LMAX : (j + 1) * LMAX] = (live * block).astype(BF16)


def middle_kernel(
    core_ref,
    tokens_ref,
    attended_ref,
    own_ref,
    other_ref,
    gain_ref,
    middle_ref,
    normed_ref,
    mid,
    moved,
):
    core = core_ref[0]
    low, high = attended_ref[:KHALF, :], attended_ref[KHALF:, :]
    for weights, half in ((own_ref, core), (other_ref, 1 - core)):
        for s in range(8):
            rows = dot_nn(weights[s], low) + dot_nn(weights[8 + s], high)
            start = pl.multiple_of((2 * s + half) * OW, 8)
            mid[pl.ds(start, OW), :] = rows
    total = jnp.zeros((1, LMAX), F32)
    for j in range(10):
        cols = slice(j * LMAX, (j + 1) * LMAX)
        block = mid[cols, :] + tokens_ref[:, cols].astype(F32).T
        mid[cols, :] = block
        middle_ref[:, cols] = block.T
        total = total + jnp.sum(block * block, axis=0, keepdims=True)
    scale = lax.rsqrt(total * (1.0 / D) + 1e-05)
    for j in range(16):
        for lo in range(2):
            start = lo * KHALF + j * 40
            block = mid[start : start + 40, :] * scale * gain_ref[start : start + 40, :]
            moved[j * 80 + lo * 40 : j * 80 + lo * 40 + 40, :] = block
    for j in range(10):
        cols = slice(j * LMAX, (j + 1) * LMAX)
        normed_ref[:, cols] = moved[cols, :].T.astype(BF16)


def hidden_kernel(
    own_ref, next_ref, across_ref, gate_up_ref, first_ref, second_ref, keep_ref, send_ref, tokens
):
    tokens[:LMAX, :] = own_ref[...]
    tokens[LMAX : 2 * LMAX, :] = next_ref[...]
    tokens[2 * LMAX : 3 * LMAX, :] = across_ref[0]
    tokens[3 * LMAX :, :] = across_ref[1]

    def block(start, down_ref):
        gate_up = dot_nn(tokens[...], gate_up_ref[:, start : start + 2 * UNITS])
        gate, up = gate_up[:, :WIDE], gate_up[:, WIDE : 2 * WIDE]
        units = (gate / (1.0 + jnp.exp(-gate)) * up).astype(BF16)
        gate = gate_up[:, 2 * WIDE :]
        up = pltpu.roll(gate, 64, 1)
        rest = (gate / (1.0 + jnp.exp(-gate)) * up).astype(BF16)[:, :64]
        total = dot_nn(units, down_ref[:WIDE, :]) + dot_nn(rest, down_ref[WIDE:, :])
        return total.astype(BF16).astype(F32)

    total = block(0, first_ref) + block(2 * UNITS, second_ref)
    keep_ref[0] = total[:LMAX]
    keep_ref[1] = total[LMAX : 2 * LMAX]
    send_ref[0] = total[2 * LMAX : 3 * LMAX].astype(BF16)
    send_ref[1] = total[3 * LMAX :].astype(BF16)


VMEM = pl.BlockSpec(memory_space=pltpu.VMEM)
SMEM = pl.BlockSpec(memory_space=pltpu.SMEM)


def attention(length, core, tokens, own, other, gain):
    cosine, sine = tables()
    return pl.pallas_call(
        attention_kernel,
        out_shape=(
            jax.ShapeDtypeStruct((D, LMAX), BF16),
            jax.ShapeDtypeStruct((LMAX, 640), BF16),
        ),
        in_specs=[SMEM, SMEM] + [VMEM] * 6,
        out_specs=(VMEM, VMEM),
        scratch_shapes=[pltpu.VMEM((1920, LMAX), F32)],
        compiler_params=pltpu.CompilerParams(vmem_limit_bytes=32 << 20),
        cost_estimate=pl.CostEstimate(
            flops=800000000, bytes_accessed=6000000, transcendentals=400000
        ),
        name="attention",
    )(
        length, core, tokens, own, other, jnp.asarray(cosine), jnp.asarray(sine), gain[None, :]
    )


def middle_rows(core, tokens, attended, own, other, gain):
    return pl.pallas_call(
        middle_kernel,
        out_shape=(
            jax.ShapeDtypeStruct((LMAX, D), F32),
            jax.ShapeDtypeStruct((LMAX, D), BF16),
        ),
        in_specs=[SMEM] + [VMEM] * 5,
        out_specs=(VMEM, VMEM),
        scratch_shapes=[pltpu.VMEM((D, LMAX), F32), pltpu.VMEM((D, LMAX), F32)],
        compiler_params=pltpu.CompilerParams(vmem_limit_bytes=32 << 20),
        cost_estimate=pl.CostEstimate(
            flops=420000000, bytes_accessed=4000000, transcendentals=1000
        ),
        name="middle",
    )(core, tokens, attended, own, other, gain[:, None])


def hidden_rows(own, beside, across, gate_up, down_first, down_second):
    return pl.pallas_call(
        hidden_kernel,
        out_shape=(
            jax.ShapeDtypeStruct((2, LMAX, D), F32),
            jax.ShapeDtypeStruct((2, LMAX, D), BF16),
        ),
        in_specs=[VMEM] * 6,
        out_specs=(VMEM, VMEM),
        scratch_shapes=[pltpu.VMEM((4 * LMAX, D), BF16)],
        compiler_params=pltpu.CompilerParams(vmem_limit_bytes=36 << 20),
        cost_estimate=pl.CostEstimate(
            flops=3500000000, bytes_accessed=9500000, transcendentals=500000
        ),
        name="hidden",
    )(own, beside, across, gate_up, down_first, down_second)


def turn(same_x):
    pairs = []
    for lo in range(2):
        for core in range(2):
            for hi in range(2):
                to_lo = lo if same_x else 1 - lo
                pairs.append((lo * 4 + core * 2 + hi, to_lo * 4 + hi * 2 + core))
    return pairs


def spread(block, axes, count):
    copies = jnp.broadcast_to(block[None], (count,) + block.shape)
    return lax.all_to_all(copies, axes, 0, 0, tiled=False)


def after(value, *others):
    return lax.optimization_barrier((value,) + others)[0]


SWAP = [(0, 1), (1, 0)]
BESIDE = [(y, y ^ 1) for y in range(4)]


def shards(
    prompts, lengths, qkv_master, out_master, gate_up_master, down_weight, attn_gain, mlp_gain
):
    core = lax.axis_index("core").astype(jnp.int32)
    x_lo = lax.axis_index("x_lo")
    core_at = core[None]
    tokens = prompts[0]
    gate_up = gate_up_master.astype(BF16)
    merged = jnp.concatenate(
        [
            out_master.astype(BF16),
            qkv_master.astype(BF16),
            gate_up[:, 0, :WIDE],
            gate_up[:, 1, :WIDE],
            gate_up[:, 0, WIDE:],
            gate_up[:, 1, WIDE:],
        ],
        axis=1,
    )
    merged = lax.all_gather(merged, "core", axis=0, tiled=True)
    part = jnp.concatenate(
        [
            lax.dynamic_slice_in_dim(merged[:, 160:400], core * QW, QW, axis=1),
            jnp.zeros((40, 128 - QW), BF16),
            lax.dynamic_slice_in_dim(merged[:, :160], core * OW, OW, axis=1),
            jnp.zeros((40, 128 - OW), BF16),
        ],
        axis=1,
    )
    part = spread(part, "z", 16).reshape(KHALF, 256)
    rows = merged[:, 400:]
    along = ("x_lo", "core", "x_hi")
    near = lax.ppermute(rows, along, turn(True))
    far = lax.ppermute(rows, along, turn(False))
    near = jnp.where(
        x_lo == 0, jnp.concatenate([near, far], axis=0), jnp.concatenate([far, near], axis=0)
    )
    opposite = lax.ppermute(near, "y", [(y, y ^ 2) for y in range(4)])
    gate_up_rows = lax.all_gather(
        jnp.concatenate([near, opposite], axis=1), "z", axis=0, tiled=True
    )
    down = after(down_weight, merged)
    down_first = lax.ppermute(
        down, ("core", "x_hi"), [(2 * a + b, 2 * b + a) for a in range(2) for b in range(2)]
    )
    down_second = lax.ppermute(
        down,
        ("core", "y", "x_hi"),
        [
            (8 * a + 2 * y + b, 8 * b + 2 * (y ^ 2) + a)
            for a in range(2)
            for y in range(4)
            for b in range(2)
        ],
    )
    part_qkv = after(part[:, :QW].T, near, down_first, down_second)
    qkv_own = spread(part_qkv, ("x_lo", "y", "x_hi"), 16)
    part_out = after(part[:, 128 : 128 + OW].T, qkv_own)
    out_own = spread(part_out, ("x_lo", "y", "x_hi"), 16)
    qkv_other = lax.ppermute(qkv_own, "core", SWAP)
    attended, cache = attention(lengths, core_at, tokens, qkv_own, qkv_other, attn_gain)
    out_own = after(out_own, attended)
    out_other = lax.ppermute(out_own, "core", SWAP)
    middle, normed_mid = middle_rows(core_at, tokens, attended, out_own, out_other, mlp_gain)
    beside = lax.ppermute(normed_mid, "y", BESIDE)
    across = lax.ppermute(jnp.stack([normed_mid, beside]), "core", SWAP)
    keep, send = hidden_rows(normed_mid, beside, across, gate_up_rows, down_first, down_second)
    sums = keep + lax.ppermute(send, "core", SWAP).astype(F32)
    feed_out = sums[0] + lax.ppermute(sums[1].astype(BF16), "y", BESIDE).astype(F32)
    live_rows = (jnp.arange(LMAX) < lengths[0]).astype(F32)[:, None]
    hidden = (live_rows * (middle + feed_out)).astype(BF16)
    return (hidden[None], cache[None])


def solution(mesh):
    fine = Mesh(mesh.devices.reshape(SIZES), AXES)
    group = ("x_lo", "z", "core")
    shard = ("y", "x_hi")
    in_specs = (
        P(group + shard, None, None),
        P(group + shard),
        P(group, shard),
        P(group, shard),
        P(group, None, shard),
        P(shard, None),
        P(),
        P(),
    )
    out_specs = (P(group + shard, None, None), P(group + shard, None, None))
    return jax.shard_map(shards, mesh=fine, in_specs=in_specs, out_specs=out_specs, check_vma=False)
```

```python
import jax
import jax.numpy as jnp
import numpy as np
from jax import lax
from jax.experimental import pallas as pl
from jax.experimental.pallas import tpu as pltpu
from jax.sharding import Mesh, PartitionSpec as P

QUERY_HEADS = 20
KEY_VALUE_HEADS = 5
HEAD_SIZE = 64
D = 1280
LMAX = 128
QW = 120
OW = 80
KHALF = 640
UNITS = 448
WIDE = 384
F32 = jnp.float32
BF16 = jnp.bfloat16

AXES = ("x_lo", "z", "core", "y", "x_hi")
SIZES = (2, 16, 2, 4, 2)


def tables():
    half_dim = HEAD_SIZE // 2
    frequency = np.float32(10000.0) ** (
        -(np.arange(half_dim).astype(np.float32) * np.float32(2.0) / np.float32(HEAD_SIZE))
    )
    angles = frequency.astype(np.float32)[:, None] * np.arange(LMAX).astype(np.float32)[None, :]
    return np.cos(angles).astype(np.float32), np.sin(angles).astype(np.float32)


def dot_nt(left, right):
    return lax.dot_general(left, right, (((1,), (1,)), ((), ())), preferred_element_type=F32)


def dot_nn(left, right):
    return jnp.dot(left, right, preferred_element_type=F32)


def attention_kernel(
    length_ref,
    core_ref,
    tokens_ref,
    own_ref,
    other_ref,
    cos_ref,
    sin_ref,
    gain_ref,
    attended_ref,
    cache_ref,
    qkv,
):
    length = length_ref[0]
    core = core_ref[0]
    stream = tokens_ref[...].astype(F32)
    square = jnp.mean(stream * stream, axis=-1, keepdims=True)
    normed = (stream * lax.rsqrt(square + 1e-05) * gain_ref[...]).astype(BF16)
    low, high = normed[:, :KHALF], normed[:, KHALF:]
    for weights, half in ((own_ref, core), (other_ref, 1 - core)):
        for s in range(8):
            rows = dot_nt(weights[s], low) + dot_nt(weights[8 + s], high)
            start = pl.multiple_of((2 * s + half) * QW, 8)
            qkv[pl.ds(start, QW), :] = rows.astype(BF16).astype(F32)
    cosine = cos_ref[...]
    sine = sin_ref[...]

    def rotate(start):
        first = qkv[start : start + 32, :]
        second = qkv[start + 32 : start + 64, :]
        return jnp.concatenate(
            [first * cosine - second * sine, second * cosine + first * sine], axis=0
        )

    key_at = lax.broadcasted_iota(jnp.int32, (LMAX, LMAX), 0)
    query_at = lax.broadcasted_iota(jnp.int32, (LMAX, LMAX), 1)
    allowed = (key_at <= query_at) & (key_at < length)
    allowed = jnp.concatenate([allowed.astype(F32)] * 4, axis=1) > 0.5
    for g in range(KEY_VALUE_HEADS):
        key_start = (QUERY_HEADS + g) * HEAD_SIZE
        value_start = (QUERY_HEADS + KEY_VALUE_HEADS + g) * HEAD_SIZE
        keys = rotate(key_start).astype(BF16).astype(F32)
        qkv[key_start : key_start + HEAD_SIZE, :] = keys
        keys = keys.T.astype(BF16)
        values = qkv[value_start : value_start + HEAD_SIZE, :].astype(BF16)
        queries = jnp.concatenate(
            [rotate((4 * g + h) * HEAD_SIZE).astype(BF16) for h in range(4)], axis=1
        )
        scores = dot_nn(keys, queries) * HEAD_SIZE ** (-0.5)
        scores = jnp.where(allowed, scores, -1e30)
        weights = jnp.exp(scores - jnp.max(scores, axis=0, keepdims=True))
        probability = (weights / jnp.sum(weights, axis=0, keepdims=True)).astype(BF16)
        out = dot_nn(values, probability).astype(BF16)
        for h in range(4):
            row = (4 * g + h) * HEAD_SIZE
            attended_ref[row : row + HEAD_SIZE, :] = out[:, h * LMAX : (h + 1) * LMAX]
    live = (lax.broadcasted_iota(jnp.int32, (LMAX, LMAX), 0) < length).astype(F32)
    for j in range(5):
        row = QUERY_HEADS * HEAD_SIZE + j * LMAX
        block = qkv[row : row + LMAX, :].T
        cache_ref[:, j * LMAX : (j + 1) * LMAX] = (live * block).astype(BF16)


def middle_kernel(
    core_ref,
    tokens_ref,
    attended_ref,
    own_ref,
    other_ref,
    gain_ref,
    middle_ref,
    normed_ref,
    mid,
    moved,
):
    core = core_ref[0]
    low, high = attended_ref[:KHALF, :], attended_ref[KHALF:, :]
    for weights, half in ((own_ref, core), (other_ref, 1 - core)):
        for s in range(8):
            rows = dot_nn(weights[s], low) + dot_nn(weights[8 + s], high)
            start = pl.multiple_of((2 * s + half) * OW, 8)
            mid[pl.ds(start, OW), :] = rows
    total = jnp.zeros((1, LMAX), F32)
    for j in range(10):
        cols = slice(j * LMAX, (j + 1) * LMAX)
        block = mid[cols, :] + tokens_ref[:, cols].astype(F32).T
        mid[cols, :] = block
        middle_ref[:, cols] = block.T
        total = total + jnp.sum(block * block, axis=0, keepdims=True)
    scale = lax.rsqrt(total * (1.0 / D) + 1e-05)
    for j in range(16):
        for lo in range(2):
            start = lo * KHALF + j * 40
            block = mid[start : start + 40, :] * scale * gain_ref[start : start + 40, :]
            moved[j * 80 + lo * 40 : j * 80 + lo * 40 + 40, :] = block
    for j in range(10):
        cols = slice(j * LMAX, (j + 1) * LMAX)
        normed_ref[:, cols] = moved[cols, :].T.astype(BF16)


def hidden_kernel(
    own_ref, next_ref, across_ref, gate_up_ref, first_ref, second_ref, keep_ref, send_ref, tokens
):
    tokens[:LMAX, :] = own_ref[...]
    tokens[LMAX : 2 * LMAX, :] = next_ref[...]
    tokens[2 * LMAX : 3 * LMAX, :] = across_ref[0]
    tokens[3 * LMAX :, :] = across_ref[1]

    def block(start, down_ref):
        gate_up = dot_nn(tokens[...], gate_up_ref[:, start : start + 2 * UNITS])
        gate, up = gate_up[:, :WIDE], gate_up[:, WIDE : 2 * WIDE]
        units = (gate / (1.0 + jnp.exp(-gate)) * up).astype(BF16)
        gate = gate_up[:, 2 * WIDE :]
        up = pltpu.roll(gate, 64, 1)
        rest = (gate / (1.0 + jnp.exp(-gate)) * up).astype(BF16)[:, :64]
        total = dot_nn(units, down_ref[:WIDE, :]) + dot_nn(rest, down_ref[WIDE:, :])
        return total.astype(BF16).astype(F32)

    total = block(0, first_ref) + block(2 * UNITS, second_ref)
    keep_ref[0] = total[:LMAX]
    keep_ref[1] = total[LMAX : 2 * LMAX]
    send_ref[0] = total[2 * LMAX : 3 * LMAX].astype(BF16)
    send_ref[1] = total[3 * LMAX :].astype(BF16)


VMEM = pl.BlockSpec(memory_space=pltpu.VMEM)
SMEM = pl.BlockSpec(memory_space=pltpu.SMEM)


def attention(length, core, tokens, own, other, gain):
    cosine, sine = tables()
    return pl.pallas_call(
        attention_kernel,
        out_shape=(
            jax.ShapeDtypeStruct((D, LMAX), BF16),
            jax.ShapeDtypeStruct((LMAX, 640), BF16),
        ),
        in_specs=[SMEM, SMEM] + [VMEM] * 6,
        out_specs=(VMEM, VMEM),
        scratch_shapes=[pltpu.VMEM((1920, LMAX), F32)],
        compiler_params=pltpu.CompilerParams(vmem_limit_bytes=32 << 20),
        cost_estimate=pl.CostEstimate(
            flops=800000000, bytes_accessed=6000000, transcendentals=400000
        ),
        name="attention",
    )(
        length, core, tokens, own, other, jnp.asarray(cosine), jnp.asarray(sine), gain[None, :]
    )


def middle_rows(core, tokens, attended, own, other, gain):
    return pl.pallas_call(
        middle_kernel,
        out_shape=(
            jax.ShapeDtypeStruct((LMAX, D), F32),
            jax.ShapeDtypeStruct((LMAX, D), BF16),
        ),
        in_specs=[SMEM] + [VMEM] * 5,
        out_specs=(VMEM, VMEM),
        scratch_shapes=[pltpu.VMEM((D, LMAX), F32), pltpu.VMEM((D, LMAX), F32)],
        compiler_params=pltpu.CompilerParams(vmem_limit_bytes=32 << 20),
        cost_estimate=pl.CostEstimate(
            flops=420000000, bytes_accessed=4000000, transcendentals=1000
        ),
        name="middle",
    )(core, tokens, attended, own, other, gain[:, None])


def hidden_rows(own, beside, across, gate_up, down_first, down_second):
    return pl.pallas_call(
        hidden_kernel,
        out_shape=(
            jax.ShapeDtypeStruct((2, LMAX, D), F32),
            jax.ShapeDtypeStruct((2, LMAX, D), BF16),
        ),
        in_specs=[VMEM] * 6,
        out_specs=(VMEM, VMEM),
        scratch_shapes=[pltpu.VMEM((4 * LMAX, D), BF16)],
        compiler_params=pltpu.CompilerParams(vmem_limit_bytes=36 << 20),
        cost_estimate=pl.CostEstimate(
            flops=3500000000, bytes_accessed=9500000, transcendentals=500000
        ),
        name="hidden",
    )(own, beside, across, gate_up, down_first, down_second)


def spread(block, axes, count):
    copies = jnp.broadcast_to(block[None], (count,) + block.shape)
    return lax.all_to_all(copies, axes, 0, 0, tiled=False)


def after(value, *others):
    return lax.optimization_barrier((value,) + others)[0]


SWAP = [(0, 1), (1, 0)]
BESIDE = [(0, 3), (3, 0), (1, 2), (2, 1)]
FIRST = [(y, y) for y in range(4)] + [(4 + y, 4 + (y + 1) % 4) for y in range(4)]
SECOND = [(y, (y + 3) % 4) for y in range(4)] + [(4 + y, 4 + (y + 2) % 4) for y in range(4)]


def shards(
    prompts, lengths, qkv_master, out_master, gate_up_master, down_weight, attn_gain, mlp_gain
):
    core = lax.axis_index("core").astype(jnp.int32)
    x_lo = lax.axis_index("x_lo")
    core_at = core[None]
    tokens = prompts[0]
    gate_up = gate_up_master.astype(BF16)
    merged = jnp.concatenate(
        [
            out_master.astype(BF16),
            qkv_master.astype(BF16),
            gate_up[:, 0, :WIDE],
            gate_up[:, 1, :WIDE],
            gate_up[:, 0, WIDE:],
            gate_up[:, 1, WIDE:],
        ],
        axis=1,
    )
    merged = lax.all_gather(merged, "core", axis=0, tiled=True)
    part = jnp.concatenate(
        [
            lax.dynamic_slice_in_dim(merged[:, 160:400], core * QW, QW, axis=1),
            jnp.zeros((40, 128 - QW), BF16),
            lax.dynamic_slice_in_dim(merged[:, :160], core * OW, OW, axis=1),
            jnp.zeros((40, 128 - OW), BF16),
        ],
        axis=1,
    )
    part = spread(part, "z", 16).reshape(KHALF, 256)
    rows = merged[:, 400:]
    far = lax.ppermute(rows, "x_lo", SWAP)
    rows = jnp.where(
        x_lo == 0, jnp.concatenate([rows, far], axis=0), jnp.concatenate([far, rows], axis=0)
    )
    first = lax.ppermute(rows, ("core", "y"), FIRST)
    second = lax.ppermute(rows, ("core", "y"), SECOND)
    gate_up_rows = lax.all_gather(
        jnp.concatenate([first, second], axis=1), "z", axis=0, tiled=True
    )
    down_first = lax.ppermute(down_weight, ("core", "y"), FIRST)
    down_second = lax.ppermute(down_weight, ("core", "y"), SECOND)
    part_qkv = after(part[:, :QW].T, first)
    qkv_own = spread(part_qkv, ("x_lo", "y", "x_hi"), 16)
    copies = jnp.broadcast_to(part[:, 128 : 128 + OW].T[None], (16, OW, KHALF))
    copies = after(copies, qkv_own)
    out_own = lax.all_to_all(copies, ("x_lo", "y", "x_hi"), 0, 0, tiled=False)
    qkv_other = lax.ppermute(qkv_own, "core", SWAP)
    attended, cache = attention(lengths, core_at, tokens, qkv_own, qkv_other, attn_gain)
    out_own = after(out_own, attended, down_first, down_second)
    out_other = lax.ppermute(out_own, "core", SWAP)
    middle, normed_mid = middle_rows(core_at, tokens, attended, out_own, out_other, mlp_gain)
    beside = lax.ppermute(normed_mid, ("x_lo", "x_hi"), BESIDE)
    across = lax.ppermute(jnp.stack([normed_mid, beside]), "core", SWAP)
    keep, send = hidden_rows(normed_mid, beside, across, gate_up_rows, down_first, down_second)
    sums = keep + lax.ppermute(send, "core", SWAP).astype(F32)
    feed_out = sums[0] + lax.ppermute(
        sums[1].astype(BF16), ("x_lo", "x_hi"), BESIDE
    ).astype(F32)
    live_rows = (jnp.arange(LMAX) < lengths[0]).astype(F32)[:, None]
    hidden = (live_rows * (middle + feed_out)).astype(BF16)
    return (hidden[None], cache[None])


def solution(mesh):
    fine = Mesh(mesh.devices.reshape(SIZES), AXES)
    group = ("x_lo", "z", "core")
    shard = ("y", "x_hi")
    in_specs = (
        P(group + shard, None, None),
        P(group + shard),
        P(group, shard),
        P(group, shard),
        P(group, None, shard),
        P(shard, None),
        P(),
        P(),
    )
    out_specs = (P(group + shard, None, None), P(group + shard, None, None))
    return jax.shard_map(shards, mesh=fine, in_specs=in_specs, out_specs=out_specs, check_vma=False)
```

```python
import jax
import jax.numpy as jnp
import numpy as np
from jax import lax
from jax.experimental import pallas as pl
from jax.experimental.pallas import tpu as pltpu
from jax.sharding import Mesh, PartitionSpec as P

QUERY_HEADS = 20
KEY_VALUE_HEADS = 5
HEAD_SIZE = 64
D = 1280
LMAX = 128
QW = 120
OW = 80
KHALF = 640
UNITS = 448
WIDE = 384
F32 = jnp.float32
BF16 = jnp.bfloat16

AXES = ("x_lo", "z", "core", "y", "x_hi")
SIZES = (2, 16, 2, 4, 2)


def tables():
    half_dim = HEAD_SIZE // 2
    frequency = np.float32(10000.0) ** (
        -(np.arange(half_dim).astype(np.float32) * np.float32(2.0) / np.float32(HEAD_SIZE))
    )
    angles = frequency.astype(np.float32)[:, None] * np.arange(LMAX).astype(np.float32)[None, :]
    return np.cos(angles).astype(np.float32), np.sin(angles).astype(np.float32)


def dot_nt(left, right):
    return lax.dot_general(left, right, (((1,), (1,)), ((), ())), preferred_element_type=F32)


def dot_nn(left, right):
    return jnp.dot(left, right, preferred_element_type=F32)


def attention_kernel(
    length_ref,
    core_ref,
    tokens_ref,
    own_ref,
    other_ref,
    cos_ref,
    sin_ref,
    gain_ref,
    attended_ref,
    cache_ref,
    qkv,
):
    length = length_ref[0]
    core = core_ref[0]
    stream = tokens_ref[...].astype(F32)
    square = jnp.mean(stream * stream, axis=-1, keepdims=True)
    normed = (stream * lax.rsqrt(square + 1e-05) * gain_ref[...]).astype(BF16)
    low, high = normed[:, :KHALF], normed[:, KHALF:]
    for weights, half in ((own_ref, core), (other_ref, 1 - core)):
        for s in range(8):
            rows = dot_nt(weights[s], low) + dot_nt(weights[8 + s], high)
            start = pl.multiple_of((2 * s + half) * QW, 8)
            qkv[pl.ds(start, QW), :] = rows.astype(BF16).astype(F32)
    cosine = cos_ref[...]
    sine = sin_ref[...]

    def rotate(start):
        first = qkv[start : start + 32, :]
        second = qkv[start + 32 : start + 64, :]
        return jnp.concatenate(
            [first * cosine - second * sine, second * cosine + first * sine], axis=0
        )

    key_at = lax.broadcasted_iota(jnp.int32, (LMAX, LMAX), 0)
    query_at = lax.broadcasted_iota(jnp.int32, (LMAX, LMAX), 1)
    allowed = (key_at <= query_at) & (key_at < length)
    allowed = jnp.concatenate([allowed.astype(F32)] * 4, axis=1) > 0.5
    for g in range(KEY_VALUE_HEADS):
        key_start = (QUERY_HEADS + g) * HEAD_SIZE
        value_start = (QUERY_HEADS + KEY_VALUE_HEADS + g) * HEAD_SIZE
        keys = rotate(key_start).astype(BF16).astype(F32)
        qkv[key_start : key_start + HEAD_SIZE, :] = keys
        keys = keys.T.astype(BF16)
        values = qkv[value_start : value_start + HEAD_SIZE, :].astype(BF16)
        queries = jnp.concatenate(
            [rotate((4 * g + h) * HEAD_SIZE).astype(BF16) for h in range(4)], axis=1
        )
        scores = dot_nn(keys, queries) * HEAD_SIZE ** (-0.5)
        scores = jnp.where(allowed, scores, -1e30)
        weights = jnp.exp(scores - jnp.max(scores, axis=0, keepdims=True))
        probability = (weights / jnp.sum(weights, axis=0, keepdims=True)).astype(BF16)
        out = dot_nn(values, probability).astype(BF16)
        for h in range(4):
            row = (4 * g + h) * HEAD_SIZE
            attended_ref[row : row + HEAD_SIZE, :] = out[:, h * LMAX : (h + 1) * LMAX]
    live = (lax.broadcasted_iota(jnp.int32, (LMAX, LMAX), 0) < length).astype(F32)
    for j in range(5):
        row = QUERY_HEADS * HEAD_SIZE + j * LMAX
        block = qkv[row : row + LMAX, :].T
        cache_ref[:, j * LMAX : (j + 1) * LMAX] = (live * block).astype(BF16)


def middle_kernel(
    core_ref,
    tokens_ref,
    attended_ref,
    own_ref,
    other_ref,
    gain_ref,
    middle_ref,
    normed_ref,
    mid,
    moved,
):
    core = core_ref[0]
    low, high = attended_ref[:KHALF, :], attended_ref[KHALF:, :]
    for weights, half in ((own_ref, core), (other_ref, 1 - core)):
        for s in range(8):
            rows = dot_nn(weights[s], low) + dot_nn(weights[8 + s], high)
            start = pl.multiple_of((2 * s + half) * OW, 8)
            mid[pl.ds(start, OW), :] = rows
    total = jnp.zeros((1, LMAX), F32)
    for j in range(10):
        cols = slice(j * LMAX, (j + 1) * LMAX)
        block = mid[cols, :] + tokens_ref[:, cols].astype(F32).T
        mid[cols, :] = block
        middle_ref[:, cols] = block.T
        total = total + jnp.sum(block * block, axis=0, keepdims=True)
    scale = lax.rsqrt(total * (1.0 / D) + 1e-05)
    for j in range(16):
        for lo in range(2):
            start = lo * KHALF + j * 40
            block = mid[start : start + 40, :] * scale * gain_ref[start : start + 40, :]
            moved[j * 80 + lo * 40 : j * 80 + lo * 40 + 40, :] = block
    for j in range(10):
        cols = slice(j * LMAX, (j + 1) * LMAX)
        normed_ref[:, cols] = moved[cols, :].T.astype(BF16)


def hidden_kernel(
    own_ref, next_ref, across_ref, gate_up_ref, first_ref, second_ref, keep_ref, send_ref, tokens
):
    tokens[:LMAX, :] = own_ref[...]
    tokens[LMAX : 2 * LMAX, :] = next_ref[...]
    tokens[2 * LMAX : 3 * LMAX, :] = across_ref[0]
    tokens[3 * LMAX :, :] = across_ref[1]

    def block(start, down_ref):
        gate_up = dot_nn(tokens[...], gate_up_ref[:, start : start + 2 * UNITS])
        gate, up = gate_up[:, :WIDE], gate_up[:, WIDE : 2 * WIDE]
        units = (gate / (1.0 + jnp.exp(-gate)) * up).astype(BF16)
        gate = gate_up[:, 2 * WIDE :]
        up = pltpu.roll(gate, 64, 1)
        rest = (gate / (1.0 + jnp.exp(-gate)) * up).astype(BF16)[:, :64]
        total = dot_nn(units, down_ref[:WIDE, :]) + dot_nn(rest, down_ref[WIDE:, :])
        return total.astype(BF16).astype(F32)

    total = block(0, first_ref) + block(2 * UNITS, second_ref)
    keep_ref[0] = total[:LMAX]
    keep_ref[1] = total[LMAX : 2 * LMAX]
    send_ref[0] = total[2 * LMAX : 3 * LMAX].astype(BF16)
    send_ref[1] = total[3 * LMAX :].astype(BF16)


VMEM = pl.BlockSpec(memory_space=pltpu.VMEM)
SMEM = pl.BlockSpec(memory_space=pltpu.SMEM)


def attention(length, core, tokens, own, other, gain):
    cosine, sine = tables()
    return pl.pallas_call(
        attention_kernel,
        out_shape=(
            jax.ShapeDtypeStruct((D, LMAX), BF16),
            jax.ShapeDtypeStruct((LMAX, 640), BF16),
        ),
        in_specs=[SMEM, SMEM] + [VMEM] * 6,
        out_specs=(VMEM, VMEM),
        scratch_shapes=[pltpu.VMEM((1920, LMAX), F32)],
        compiler_params=pltpu.CompilerParams(vmem_limit_bytes=16 << 20),
        cost_estimate=pl.CostEstimate(
            flops=800000000, bytes_accessed=6000000, transcendentals=400000
        ),
        name="attention",
    )(
        length, core, tokens, own, other, jnp.asarray(cosine), jnp.asarray(sine), gain[None, :]
    )


def middle_rows(core, tokens, attended, own, other, gain):
    return pl.pallas_call(
        middle_kernel,
        out_shape=(
            jax.ShapeDtypeStruct((LMAX, D), F32),
            jax.ShapeDtypeStruct((LMAX, D), BF16),
        ),
        in_specs=[SMEM] + [VMEM] * 5,
        out_specs=(VMEM, VMEM),
        scratch_shapes=[pltpu.VMEM((D, LMAX), F32), pltpu.VMEM((D, LMAX), F32)],
        compiler_params=pltpu.CompilerParams(vmem_limit_bytes=16 << 20),
        cost_estimate=pl.CostEstimate(
            flops=420000000, bytes_accessed=4000000, transcendentals=1000
        ),
        name="middle",
    )(core, tokens, attended, own, other, gain[:, None])


def hidden_rows(own, beside, across, gate_up, down_first, down_second):
    return pl.pallas_call(
        hidden_kernel,
        out_shape=(
            jax.ShapeDtypeStruct((2, LMAX, D), F32),
            jax.ShapeDtypeStruct((2, LMAX, D), BF16),
        ),
        in_specs=[VMEM] * 6,
        out_specs=(VMEM, VMEM),
        scratch_shapes=[pltpu.VMEM((4 * LMAX, D), BF16)],
        compiler_params=pltpu.CompilerParams(vmem_limit_bytes=24 << 20),
        cost_estimate=pl.CostEstimate(
            flops=3500000000, bytes_accessed=9500000, transcendentals=500000
        ),
        name="hidden",
    )(own, beside, across, gate_up, down_first, down_second)


def spread(block, axes, count):
    copies = jnp.broadcast_to(block[None], (count,) + block.shape)
    return lax.all_to_all(copies, axes, 0, 0, tiled=False)


def after(value, *others):
    return lax.optimization_barrier((value,) + others)[0]


SWAP = [(0, 1), (1, 0)]
FIRST = [(y, y) for y in range(4)] + [(4 + y, 4 + (y + 1) % 4) for y in range(4)]
SECOND = [
    (
        ((lo * 2 + core) * 4 + y) * 2 + hi,
        ((lo * 2) * 4 + (y + 3) % 4) * 2 + hi
        if core == 0
        else (((1 - lo) * 2 + 1) * 4 + y) * 2 + 1 - hi,
    )
    for lo in range(2)
    for core in range(2)
    for y in range(4)
    for hi in range(2)
]
BESIDE = [
    ((lo * 4 + y) * 2 + hi, ((1 - lo) * 4 + (y ^ 2)) * 2 + 1 - hi)
    for lo in range(2)
    for y in range(4)
    for hi in range(2)
]
PLANE = ("x_lo", "y", "x_hi")
CORES = ("x_lo", "core", "y", "x_hi")


def shards(
    prompts, lengths, qkv_master, out_master, gate_up_master, down_weight, attn_gain, mlp_gain
):
    core = lax.axis_index("core").astype(jnp.int32)
    x_lo = lax.axis_index("x_lo")
    core_at = core[None]
    tokens = prompts[0]
    gate_up = gate_up_master.astype(BF16)
    merged = jnp.concatenate(
        [
            out_master.astype(BF16),
            qkv_master.astype(BF16),
            gate_up[:, 0, :WIDE],
            gate_up[:, 1, :WIDE],
            gate_up[:, 0, WIDE:],
            gate_up[:, 1, WIDE:],
        ],
        axis=1,
    )
    merged = lax.all_gather(merged, "core", axis=0, tiled=True)
    part = jnp.concatenate(
        [
            lax.dynamic_slice_in_dim(merged[:, 160:400], core * QW, QW, axis=1),
            jnp.zeros((40, 128 - QW), BF16),
            lax.dynamic_slice_in_dim(merged[:, :160], core * OW, OW, axis=1),
            jnp.zeros((40, 128 - OW), BF16),
        ],
        axis=1,
    )
    part = spread(part, "z", 16).reshape(KHALF, 256)
    rows = merged[:, 400:]
    far = lax.ppermute(rows, "x_lo", SWAP)
    rows = jnp.where(
        x_lo == 0, jnp.concatenate([rows, far], axis=0), jnp.concatenate([far, rows], axis=0)
    )
    first = lax.ppermute(rows, ("core", "y"), FIRST)
    second = lax.ppermute(rows, CORES, SECOND)
    gate_up_rows = lax.all_gather(
        jnp.concatenate([first, second], axis=1), "z", axis=0, tiled=True
    )
    down_first = lax.ppermute(down_weight, ("core", "y"), FIRST)
    down_second = lax.ppermute(down_weight, CORES, SECOND)
    part_qkv = after(part[:, :QW].T, first)
    qkv_own = spread(part_qkv, ("x_lo", "y", "x_hi"), 16)
    copies = jnp.broadcast_to(part[:, 128 : 128 + OW].T[None], (16, OW, KHALF))
    copies = after(copies, qkv_own)
    out_own = lax.all_to_all(copies, ("x_lo", "y", "x_hi"), 0, 0, tiled=False)
    qkv_other = lax.ppermute(qkv_own, "core", SWAP)
    attended, cache = attention(lengths, core_at, tokens, qkv_own, qkv_other, attn_gain)
    out_own = after(out_own, attended, down_first, down_second)
    out_other = lax.ppermute(out_own, "core", SWAP)
    middle, normed_mid = middle_rows(core_at, tokens, attended, out_own, out_other, mlp_gain)
    beside = lax.ppermute(normed_mid, PLANE, BESIDE)
    across = lax.ppermute(jnp.stack([normed_mid, beside]), "core", SWAP)
    keep, send = hidden_rows(normed_mid, beside, across, gate_up_rows, down_first, down_second)
    sums = keep + lax.ppermute(send, "core", SWAP).astype(F32)
    feed_out = sums[0] + lax.ppermute(sums[1].astype(BF16), PLANE, BESIDE).astype(F32)
    live_rows = (jnp.arange(LMAX) < lengths[0]).astype(F32)[:, None]
    hidden = (live_rows * (middle + feed_out)).astype(BF16)
    return (hidden[None], cache[None])


def solution(mesh):
    fine = Mesh(mesh.devices.reshape(SIZES), AXES)
    group = ("x_lo", "z", "core")
    shard = ("y", "x_hi")
    in_specs = (
        P(group + shard, None, None),
        P(group + shard),
        P(group, shard),
        P(group, shard),
        P(group, None, shard),
        P(shard, None),
        P(),
        P(),
    )
    out_specs = (P(group + shard, None, None), P(group + shard, None, None))
    return jax.shard_map(shards, mesh=fine, in_specs=in_specs, out_specs=out_specs, check_vma=False)
```
